32 devices in a mesh: tm: 2 (over y), space: 16 (over z, x, core).
Axes of the slice: x: 2, y: 2, z: 4, core: 2. Of those that a mesh axis runs over, the one named last changes fastest.
Arguments:
- slice_starts: float32 [2, 2, 256, 256], P('tm', None, 'space'), may hold values from 0.2 to 1.5
- habitat: int32 [256, 256], P('space'), may hold values from 0 to 7
- capacity_table: float32 [8], replicated, may hold values from 0.5 to 3
- prey_motility: float32 [8], replicated, may hold values from 0.03 to 0.2
- predator_motility: float32 [8], replicated, may hold values from 0.03 to 0.2
Outputs:
- slice_ends: float32 [2, 2, 256, 256], P('tm', None, 'space')
The draws below stay inside these ranges and needn't reach their ends.
All inputs are finite; a program needn't handle non-finite values.
Results may differ from the reference program's by a relative error of at most 0.00002.
Values sent between devices are 32-bit elements; how exact they have to be, the bound alone decides.
No kernel may reach another device: no remote copies, remote signals or barrier semaphores. Data moves between devices by JAX's collectives and lax.ppermute only.
A program may use at most 64 MiB of HBM per device.

```python
import math
import jax
import jax.numpy as jnp

NY = 256
CLASSES = 8
SLICES = 2
NX = 256


def with_ends(result, rng, low, largest):
    extent = result.shape
    index_at = [jax.random.randint(jax.random.fold_in(rng, axis), (), 0, extent[axis]) for axis in range(len(extent))]
    result = result.at[tuple(index_at)].set(low)
    longest = extent.index(max(extent))
    index_at[longest] = (index_at[longest] + 1) % extent[longest]
    return result.at[tuple(index_at)].set(largest)


def block_levels(rng, shape, cuts, least, high):
    factor_of, own = 1.0, jax.random.fold_in(rng, 6)
    for position, shards_of in cuts:
        heights = jnp.exp(jax.random.uniform(jax.random.fold_in(own, position), (shards_of,), jnp.float32, least / len(cuts), high / len(cuts)))
        factor_of = factor_of * jnp.repeat(heights, shape[position] // shards_of).reshape([-1 if axis == position else 1 for axis in range(len(shape))])
    return factor_of


def setup_inputs(seed: int = 0) -> dict:
    seeds = jax.random.split(jax.random.key(seed), 6)
    slice_starts = jnp.clip(0.2 + 1.3 * jax.random.uniform(seeds[0], (SLICES, 2, NX, NY), jnp.float32) ** block_levels(seeds[0], (SLICES, 2, NX, NY), ((0, 2), (2, 16)), -0.2, 0.2), 0.2, 1.5)
    habitat = with_ends(jax.random.randint(seeds[1], (NX, NY), 0, CLASSES), jax.random.fold_in(seeds[1], 1), 0, CLASSES - 1).astype(jnp.int32)
    capacity_table = jnp.clip(jnp.exp(jax.random.uniform(seeds[2], (CLASSES,), jnp.float32, math.log(0.5), math.log(3.0))), 0.5, 3.0)
    prey_motility = jnp.clip(jnp.exp(jax.random.uniform(seeds[3], (CLASSES,), jnp.float32, math.log(0.03), math.log(0.2))), 0.03, 0.2)
    predator_motility = jnp.clip(jnp.exp(jax.random.uniform(seeds[4], (CLASSES,), jnp.float32, math.log(0.03), math.log(0.2))), 0.03, 0.2)
    return dict(slice_starts=slice_starts, habitat=habitat, capacity_table=capacity_table, prey_motility=prey_motility, predator_motility=predator_motility)


GROWTH = 0.5
ATTACK = 0.5
HANDLING = 1.0
CONVERSION = 0.6
MORTALITY = 0.3
TAXIS = 0.15


def laplace(field):
    inner = field[1:-1]
    return field[2:] + field[:-2] + jnp.roll(inner, 1, -1) + jnp.roll(inner, -1, -1) - 4.0 * inner


def advance(prey, predator, prey_mob, pred_mob, capacity, step_dt, inv_h2):
    spread_prey = laplace(prey_mob * prey) * inv_h2
    spread_pred = laplace(pred_mob * predator) * inv_h2
    row_flux = 0.5 * (predator[1:] + predator[:-1]) * (prey[1:] - prey[:-1])
    inner_prey = prey[1:-1]
    inner_pred = predator[1:-1]
    col_flux = 0.5 * (inner_pred + jnp.roll(inner_pred, -1, -1)) * (jnp.roll(inner_prey, -1, -1) - inner_prey)
    taxis_div = (row_flux[1:] - row_flux[:-1] + col_flux - jnp.roll(col_flux, 1, -1)) * inv_h2
    response = inner_prey * inner_pred / (1.0 + HANDLING * jnp.abs(inner_prey))
    new_prey = inner_prey + step_dt * (spread_prey + GROWTH * inner_prey * (1.0 - inner_prey / capacity) - ATTACK * response)
    new_pred = inner_pred + step_dt * (spread_pred - TAXIS * taxis_div + CONVERSION * ATTACK * response - MORTALITY * inner_pred)
    return jnp.stack([new_prey, new_pred])


def restrict(field):
    shape = field.shape
    blocks = field.reshape(shape[:-2] + (shape[-2] // 2, 2, shape[-1] // 2, 2))
    return (blocks[..., 0, :, 0] + blocks[..., 0, :, 1] + blocks[..., 1, :, 0] + blocks[..., 1, :, 1]) * 0.25


def prolong(field):
    return jnp.repeat(jnp.repeat(field, 2, axis=-2), 2, axis=-1)


def pad_rows(field, width):
    return jnp.concatenate([field[..., -width:, :], field, field[..., :width, :]], axis=-2)


def reference(slice_starts, habitat, capacity_table, prey_motility, predator_motility):
    coefficients = jnp.stack([prey_motility[habitat], predator_motility[habitat], capacity_table[habitat]])
    coef_padded = pad_rows(coefficients, 2)
    coarse_coef = restrict(coef_padded)

    def fine_pair(fine_state):
        for sweep in range(2):
            padded = pad_rows(fine_state, 1)
            fine_state = advance(padded[0], padded[1], coef_padded[0, 1:-1], coef_padded[1, 1:-1], coef_padded[2, 2:-2], 1.0, 1.0)
        return fine_state

    def coarse_prop(fine_state):
        padded = pad_rows(restrict(fine_state), 1)
        return prolong(advance(padded[0], padded[1], coarse_coef[0], coarse_coef[1], coarse_coef[2, 1:-1], 2.0, 0.25))

    corrections = [fine_pair(slice_starts[n]) - coarse_prop(slice_starts[n]) for n in range(SLICES)]
    current = slice_starts[0]
    results = []
    for n in range(SLICES):
        current = coarse_prop(current) + corrections[n]
        results.append(current)
    return jnp.stack(results)
```

```python
import functools

import jax
import jax.numpy as jnp
from jax import lax
from jax.experimental import pallas as pl
from jax.experimental.pallas import tpu as pltpu
from jax.sharding import PartitionSpec as P

GROWTH = 0.5
ATTACK = 0.5
HANDLING = 1.0
CONVERSION = 0.6
MORTALITY = 0.3
TAXIS = 0.15

EDGE = 4
TILE = 8


def at(field, by, axis):
    return pltpu.roll(field, (-by) % field.shape[axis], axis)


def laplace(field, by):
    return (
        at(field, by, 0) + at(field, -by, 0) + at(field, by, 1) + at(field, -by, 1) - 4.0 * field
    )


def advance(state, coefs, step_dt, inv_h2, by):
    prey, predator = state
    prey_mob, pred_mob, capacity = coefs
    spread_prey = laplace(prey_mob * prey, by) * inv_h2
    spread_pred = laplace(pred_mob * predator, by) * inv_h2
    row_flux = 0.5 * (predator + at(predator, by, 0)) * (at(prey, by, 0) - prey)
    col_flux = 0.5 * (predator + at(predator, by, 1)) * (at(prey, by, 1) - prey)
    taxis_div = (row_flux - at(row_flux, -by, 0) + col_flux - at(col_flux, -by, 1)) * inv_h2
    response = prey * predator / (1.0 + HANDLING * jnp.abs(prey))
    new_prey = prey + step_dt * (
        spread_prey + GROWTH * prey * (1.0 - prey / capacity) - ATTACK * response
    )
    new_pred = predator + step_dt * (
        spread_pred - TAXIS * taxis_div + CONVERSION * ATTACK * response - MORTALITY * predator
    )
    return new_prey, new_pred


def block_mean(field):
    for axis in (0, 1):
        even = lax.broadcasted_iota(jnp.int32, field.shape, axis) % 2 == 0
        field = field + jnp.where(even, at(field, 1, axis), at(field, -1, axis))
    return field * 0.25


def fine_pair(state, coefs):
    for _ in range(2):
        state = advance(state, coefs, 1.0, 1.0, 1)
    return state


def coarse_prop(state, coarse_coefs):
    return advance(tuple(map(block_mean, state)), coarse_coefs, 2.0, 0.25, 2)


def edge_tile(strip):
    head = lax.broadcasted_iota(jnp.int32, (TILE, strip.shape[1]), 0) < EDGE
    return jnp.where(head, strip[:TILE], strip[strip.shape[0] - TILE :])


def widened(strip, after, before, swapped):
    head = lax.broadcasted_iota(jnp.int32, after.shape, 0) < EDGE
    if swapped:
        head = head == (lax.axis_index("space") % 2 == 0)
    return jnp.concatenate([strip, jnp.where(head, after, before)], axis=0)


def lookup(table_ref, habitat):
    result = jnp.full(habitat.shape, table_ref[0], jnp.float32)
    for klass in range(1, table_ref.shape[0]):
        result = jnp.where(habitat == klass, table_ref[klass], result)
    return result


def edges_kernel(*refs):
    *strips, out_ref = refs
    place = 0
    for ref in strips:
        for k in range(ref.shape[1] if len(ref.shape) == 4 else 1):
            strip = ref[0, k] if len(ref.shape) == 4 else ref[...]
            out_ref[place] = edge_tile(strip).astype(jnp.float32)
            place += 1


def strip_kernel(
    own_ref,
    prev_ref,
    habitat_ref,
    after_ref,
    before_ref,
    prey_ref,
    pred_ref,
    cap_ref,
    end_ref,
    *correction_refs,
    swapped,
):
    def wide(strip, k):
        return widened(strip, after_ref[k], before_ref[k], swapped)

    own = tuple(wide(own_ref[0, k], k) for k in range(2))
    prev = tuple(wide(prev_ref[0, k], 2 + k) for k in range(2))
    habitat = wide(habitat_ref[...].astype(jnp.float32), 4)
    coefs = tuple(lookup(ref, habitat) for ref in (prey_ref, pred_ref, cap_ref))
    coarse_coefs = tuple(map(block_mean, coefs))

    def corrections(start):
        coarse = coarse_prop(start, coarse_coefs)
        return coarse, tuple(f - g for f, g in zip(fine_pair(start, coefs), coarse))

    own_coarse, correction = corrections(own)
    prev_coarse, prev_correction = corrections(prev)
    first_end = tuple(g + c for g, c in zip(prev_coarse, prev_correction))
    handed = coarse_prop(first_end, coarse_coefs)
    first = lax.axis_index("tm") == 0
    rows = habitat_ref.shape[0]
    for k in range(2):
        end = jnp.where(first, own_coarse[k], handed[k]) + correction[k]
        end_ref[0, k] = end[:rows]
        for ref in correction_refs:
            ref[0, k] = correction[k][:rows]


def hand_kernel(
    end_ref,
    correction_ref,
    arrived_ref,
    habitat_ref,
    after_ref,
    before_ref,
    prey_ref,
    pred_ref,
    cap_ref,
    out_ref,
    *,
    swapped,
    taker,
):
    rows = habitat_ref.shape[0]
    arrived = tuple(
        widened(arrived_ref[0, k], after_ref[k], before_ref[k], swapped) for k in range(2)
    )
    habitat = widened(habitat_ref[...].astype(jnp.float32), after_ref[2], before_ref[2], swapped)
    coefs = tuple(lookup(ref, habitat) for ref in (prey_ref, pred_ref, cap_ref))
    handed = coarse_prop(arrived, tuple(map(block_mean, coefs)))
    takes = lax.axis_index("tm") == taker
    for k in range(2):
        out_ref[0, k] = jnp.where(takes, handed[k][:rows] + correction_ref[0, k], end_ref[0, k])


def local_call(kernel, outs, arrays, tables=()):
    vmem, smem = pl.BlockSpec(memory_space=pltpu.VMEM), pl.BlockSpec(memory_space=pltpu.SMEM)
    return pl.pallas_call(
        kernel,
        out_shape=[jax.ShapeDtypeStruct(shape, jnp.float32) for shape in outs],
        in_specs=[vmem] * len(arrays) + [smem] * len(tables),
        out_specs=[vmem] * len(outs),
        compiler_params=pltpu.CompilerParams(vmem_limit_bytes=4 * 2**20),
    )(*arrays, *tables)


def both_neighbours(tile):
    count = lax.axis_size("space")
    ring = [(i, (i + 1) % count) for i in range(count)]
    if count % 2:
        return (
            lax.ppermute(tile, "space", [(j, i) for i, j in ring]),
            lax.ppermute(tile, "space", ring),
            False,
        )
    swaps = [[pair for i, j in ring[start::2] for pair in ((i, j), (j, i))] for start in (0, 1)]
    outer = lax.ppermute(tile, "space", swaps[1])
    inner = lax.ppermute(tile, "space", swaps[0])
    return inner, outer, True


def from_behind(array):
    count = lax.axis_size("tm")
    return lax.ppermute(array, "tm", [(i, i + 1) for i in range(count - 1)])


def on_device(slice_starts, habitat, capacity_table, prey_motility, predator_motility):
    shape = slice_starts.shape
    tables = prey_motility, predator_motility, capacity_table
    slices = lax.axis_size("tm")
    previous = from_behind(slice_starts)
    (edges,) = local_call(
        edges_kernel, [(5, TILE, shape[-1])], [slice_starts, previous, habitat]
    )
    after, before, swapped = both_neighbours(edges)
    end, *correction = local_call(
        functools.partial(strip_kernel, swapped=swapped),
        [shape] * (1 if slices <= 2 else 2),
        [slice_starts, previous, habitat, after, before],
        tables,
    )
    for taker in range(2, slices):
        arrived = from_behind(end)
        (edges,) = local_call(edges_kernel, [(3, TILE, shape[-1])], [arrived, habitat])
        after, before, swapped = both_neighbours(edges)
        (end,) = local_call(
            functools.partial(hand_kernel, swapped=swapped, taker=taker),
            [shape],
            [end, *correction, arrived, habitat, after, before],
            tables,
        )
    return end


def solution(mesh):
    placed = (P("tm", None, "space", None), P("space", None), P(), P(), P())
    return jax.shard_map(
        on_device,
        mesh=mesh,
        in_specs=placed,
        out_specs=P("tm", None, "space", None),
        check_vma=False,
    )
```

```python
import functools

import jax
import jax.numpy as jnp
from jax import lax
from jax.experimental import pallas as pl
from jax.experimental.pallas import tpu as pltpu
from jax.sharding import PartitionSpec as P

GROWTH = 0.5
ATTACK = 0.5
HANDLING = 1.0
CONVERSION = 0.6
MORTALITY = 0.3
TAXIS = 0.15

EDGE = 4
TILE = 8
FINE = (1.0, 1.0)
COARSE = (2.0, 0.25)


def lanes(shape):
    return lax.broadcasted_iota(jnp.int32, shape, len(shape) - 1)


def take(field, index):
    return jnp.take_along_axis(field, index, axis=1, mode="promise_in_bounds")


def split(field):
    half = field.shape[1] // 2
    low, high = field[:, :half], field[:, half:]
    lane = lanes(low.shape)
    source = (2 * lane) % half
    return tuple(
        jnp.where(lane < half // 2, take(low, source + odd), take(high, source + odd))
        for odd in (0, 1)
    )


def joined(even, odd):
    half = even.shape[1]
    lane = lanes(even.shape)
    parts = []
    for first in (0, half // 2):
        source = lane // 2 + first
        part = take(even, source)
        if odd is not even:
            part = jnp.where(lane % 2 == 0, part, take(odd, source))
        parts.append(part)
    return jnp.concatenate(parts, axis=1)


def each(function, *fields):
    return tuple(map(function, *fields))


def shift(array, by, axis):
    return pltpu.roll(array, (-by) % array.shape[axis], axis)


def following(field):
    return (*field[1:], shift(field[0], 1, 1))


def preceding(field):
    return (shift(field[-1], -1, 1), *field[:-1])


def laplace(field, by):
    return each(
        lambda c, n, p: (shift(c, by, 0) + shift(c, -by, 0)) + (n + p) - 4.0 * c,
        field,
        following(field),
        preceding(field),
    )


def advance(prey, predator, prey_mob, pred_mob, inv_capacity, scales):
    step_dt, inv_h2 = scales
    by = 3 - len(prey)
    spread_prey = laplace(each(jnp.multiply, prey_mob, prey), by)
    spread_pred = laplace(each(jnp.multiply, pred_mob, predator), by)

    def flux(prey_here, pred_here, prey_next, pred_next):
        return (pred_here + pred_next) * (prey_next - prey_here)

    rows_on = [each(lambda c: shift(c, by, 0), field) for field in (prey, predator)]
    row_flux = each(flux, prey, predator, *rows_on)
    col_flux = each(flux, prey, predator, following(prey), following(predator))
    taxis_div = each(
        lambda r, c, p: (r - shift(r, -by, 0)) + (c - p), row_flux, col_flux, preceding(col_flux)
    )
    response = each(lambda u, v: u * v / (1.0 + HANDLING * jnp.abs(u)), prey, predator)
    new_prey = each(
        lambda u, s, k, r: (
            u + s + (step_dt * GROWTH) * (u * (1.0 - u * k)) - (step_dt * ATTACK) * r
        ),
        prey,
        spread_prey,
        inv_capacity,
        response,
    )
    new_pred = each(
        lambda v, s, d, r: (
            (1.0 - step_dt * MORTALITY) * v
            + s
            - (0.5 * TAXIS * step_dt * inv_h2) * d
            + (step_dt * CONVERSION * ATTACK) * r
        ),
        predator,
        spread_pred,
        taxis_div,
        response,
    )
    return new_prey, new_pred


def restrict(field):
    even, odd = field
    total = even + odd
    row = lax.broadcasted_iota(jnp.int32, total.shape, 0)
    partner = jnp.where(row % 2 == 0, shift(total, 1, 0), shift(total, -1, 0))
    return ((total + partner) * 0.25,)


def edge_tile(strip):
    head = lax.broadcasted_iota(jnp.int32, (TILE, strip.shape[1]), 0) < EDGE
    return jnp.where(head, strip[:TILE], strip[strip.shape[0] - TILE :])


def halo(after, before, swapped):
    head = lax.broadcasted_iota(jnp.int32, after.shape, 0) < EDGE
    if swapped:
        head = head == (lax.axis_index("space") % 2 == 0)
    return jnp.where(head, after, before)


def halves(array):
    half = array.shape[-1] // 2
    return array[:, :half], array[:, half:]


def load_kernel(starts_hbm, habitat_hbm, edges_ref, strip_ref, starts_ref, habitat_ref, sem):
    copies = [
        pltpu.make_async_copy(starts_hbm, starts_ref, sem.at[0]),
        pltpu.make_async_copy(habitat_hbm, habitat_ref, sem.at[1]),
    ]
    for copy in copies:
        copy.start()
    for copy in copies:
        copy.wait()
    fields = [starts_ref[0, 0], starts_ref[0, 1], habitat_ref[...].astype(jnp.float32)]
    for k, field in enumerate(fields):
        edges_ref[k] = jnp.concatenate(split(edge_tile(field)), axis=1)
        strip_ref[k] = field


def lookups(tables, habitat):
    index = habitat.astype(jnp.int32)
    return [take(jnp.broadcast_to(table[:1], index.shape), index) for table in tables]


def prepare_kernel(strip_ref, prey_ref, pred_ref, cap_ref, fields_ref, coefs_ref, tables_ref):
    lane = lanes(tables_ref.shape[1:])
    tables = []
    for ref in (prey_ref, pred_ref, cap_ref):
        table = jnp.full(lane.shape, ref[0], jnp.float32)
        for klass in range(1, ref.shape[0]):
            table = jnp.where(lane == klass, ref[klass], table)
        tables.append(table)
    tables.append(1.0 / tables[2])
    for k, table in enumerate(tables):
        tables_ref[k] = table
    half = fields_ref.shape[2] // 2
    for k in range(2):
        fields_ref[k] = jnp.concatenate(split(strip_ref[k]), axis=1)
    for part, habitat in enumerate(split(strip_ref[2])):
        for k, coef in enumerate(lookups(tables, habitat)):
            coefs_ref[k, :, part * half : (part + 1) * half] = coef


def propagate_kernel(
    fields_ref,
    coefs_ref,
    tables_ref,
    after_ref,
    before_ref,
    coarse_end_ref,
    coarse_coefs_ref,
    coarse_correction_ref,
    correction_ref,
    end_ref,
    *,
    swapped,
):
    def wide(strip, edge):
        return each(lambda *parts: jnp.concatenate(parts, axis=0), halves(strip), halves(edge))

    edges = [halo(after_ref[k], before_ref[k], swapped) for k in range(3)]
    prey, predator = (wide(fields_ref[k], edges[k]) for k in range(2))
    tables = [tables_ref[k] for k in range(4)]
    edge_coefs = zip(*(lookups(tables, part) for part in halves(edges[2])))
    coefs = [
        wide(coefs_ref[k], jnp.concatenate(edge, axis=1)) for k, edge in enumerate(edge_coefs)
    ]
    prey_mob, pred_mob, capacity, inv_capacity = coefs
    scale = COARSE[0] * COARSE[1]
    coarse_coefs = (
        each(lambda c: scale * c, restrict(prey_mob)),
        each(lambda c: scale * c, restrict(pred_mob)),
        each(lambda c: 1.0 / c, restrict(capacity)),
    )
    coarse = advance(restrict(prey), restrict(predator), *coarse_coefs, COARSE)
    fine = prey, predator
    for _ in range(2):
        fine = advance(*fine, prey_mob, pred_mob, inv_capacity, FINE)
    rows = fields_ref.shape[1]
    for k in range(2):
        correction = each(lambda f: f - coarse[k][0], fine[k])
        end = each(lambda c: coarse[k][0] + c, correction)
        coarse_end_ref[k] = restrict(end)[0]
        coarse_correction_ref[k] = restrict(correction)[0][:rows]
        correction_ref[k] = jnp.concatenate(correction, axis=1)[:rows]
        end_ref[k] = jnp.concatenate(end, axis=1)[:rows]
    for k in range(3):
        coarse_coefs_ref[k] = coarse_coefs[k][0]


def natural_kernel(correction_ref, end_ref, correction_out_ref, end_out_ref):
    for source, target in ((correction_ref, correction_out_ref), (end_ref, end_out_ref)):
        for k in range(2):
            target[0, k] = joined(*halves(source[k]))


def hand_kernel(
    arrived_ref,
    coarse_coefs_ref,
    coarse_correction_ref,
    correction_ref,
    end_ref,
    out_ref,
    *coarse_out_ref,
    taker,
):
    rows = correction_ref.shape[2]
    coarse = advance(
        *((arrived_ref[k],) for k in range(2)), *((coarse_coefs_ref[k],) for k in range(3)), COARSE
    )
    takes = lax.axis_index("tm") == taker
    for k in range(2):
        handed = coarse[k][0][:rows]
        out_ref[0, k] = jnp.where(
            takes, joined(handed, handed) + correction_ref[0, k], end_ref[0, k]
        )
        for ref in coarse_out_ref:
            ref[k] = handed + coarse_correction_ref[k]


def edges_kernel(strip_ref, out_ref):
    for k in range(strip_ref.shape[0]):
        out_ref[k] = edge_tile(strip_ref[k])


def widen_kernel(strip_ref, after_ref, before_ref, out_ref, *, swapped):
    for k in range(strip_ref.shape[0]):
        edge = halo(after_ref[k], before_ref[k], swapped)
        out_ref[k] = jnp.concatenate([strip_ref[k], edge], axis=0)


def local_call(kernel, outs, arrays, tables=(), space=pltpu.VMEM, scratch=()):
    vmem, smem = pl.BlockSpec(memory_space=pltpu.VMEM), pl.BlockSpec(memory_space=pltpu.SMEM)
    return pl.pallas_call(
        kernel,
        out_shape=[jax.ShapeDtypeStruct(shape, jnp.float32) for shape in outs],
        in_specs=[pl.BlockSpec(memory_space=space)] * len(arrays) + [smem] * len(tables),
        out_specs=[vmem] * len(outs),
        scratch_shapes=scratch,
        compiler_params=pltpu.CompilerParams(vmem_limit_bytes=4 * 2**20),
    )(*arrays, *tables)


def both_neighbours(tile):
    count = lax.axis_size("space")
    ring = [(i, (i + 1) % count) for i in range(count)]
    if count % 2:
        return (
            lax.ppermute(tile, "space", [(j, i) for i, j in ring]),
            lax.ppermute(tile, "space", ring),
            False,
        )
    swaps = [[pair for i, j in ring[start::2] for pair in ((i, j), (j, i))] for start in (0, 1)]
    outer = lax.ppermute(tile, "space", swaps[1])
    inner = lax.ppermute(tile, "space", swaps[0])
    return inner, outer, True


def from_behind(array):
    count = lax.axis_size("tm")
    return lax.ppermute(array, "tm", [(i, i + 1) for i in range(count - 1)])


def on_device(slice_starts, habitat, capacity_table, prey_motility, predator_motility):
    _, fields, rows, columns = slice_starts.shape
    wide, half = rows + TILE, columns // 2
    slices = lax.axis_size("tm")
    edges, strip = local_call(
        load_kernel,
        [(3, TILE, columns), (3, rows, columns)],
        [pltpu.with_memory_space_constraint(a, pltpu.HBM) for a in (slice_starts, habitat)],
        space=pltpu.HBM,
        scratch=[
            pltpu.VMEM(slice_starts.shape, slice_starts.dtype),
            pltpu.VMEM(habitat.shape, habitat.dtype),
            pltpu.SemaphoreType.DMA((2,)),
        ],
    )
    after, before, swapped = both_neighbours(edges)
    prepared = local_call(
        prepare_kernel,
        [(fields, rows, columns), (4, rows, columns), (4, TILE, half)],
        [strip],
        [prey_motility, predator_motility, capacity_table],
    )
    coarse_end, coarse_coefs, coarse_correction, correction, end = local_call(
        functools.partial(propagate_kernel, swapped=swapped),
        [
            (fields, wide, half),
            (3, wide, half),
            (fields, rows, half),
            (fields, rows, columns),
            (fields, rows, columns),
        ],
        [*prepared, after, before],
    )
    correction, end = local_call(
        natural_kernel, [slice_starts.shape, slice_starts.shape], [correction, end]
    )
    for taker in range(1, slices):
        arrived = from_behind(coarse_end)
        if taker > 1:
            (edges,) = local_call(edges_kernel, [(fields, TILE, half)], [arrived])
            after, before, swapped = both_neighbours(edges)
            (arrived,) = local_call(
                functools.partial(widen_kernel, swapped=swapped),
                [(fields, wide, half)],
                [arrived, after, before],
            )
        last = taker + 1 == slices
        end, *passed = local_call(
            functools.partial(hand_kernel, taker=taker),
            [slice_starts.shape] + [(fields, rows, half)] * (not last),
            [arrived, coarse_coefs, coarse_correction, correction, end],
        )
        coarse_end = None if last else passed[0]
    return end


def solution(mesh):
    placed = (P("tm", None, "space", None), P("space", None), P(), P(), P())
    return jax.shard_map(
        on_device,
        mesh=mesh,
        in_specs=placed,
        out_specs=P("tm", None, "space", None),
        check_vma=False,
    )
```

```python
import functools

import jax
import jax.numpy as jnp
from jax import lax
from jax.experimental import pallas as pl
from jax.experimental.pallas import tpu as pltpu
from jax.sharding import PartitionSpec as P

GROWTH = 0.5
ATTACK = 0.5
HANDLING = 1.0
CONVERSION = 0.6
MORTALITY = 0.3
TAXIS = 0.15

EDGE = 4
TILE = 8
FINE = (1.0, 1.0)
COARSE = (2.0, 0.25)


def lanes(shape):
    return lax.broadcasted_iota(jnp.int32, shape, len(shape) - 1)


def take(field, index):
    return jnp.take_along_axis(field, index, axis=1, mode="promise_in_bounds")


def split(field):
    half = field.shape[1] // 2
    low, high = field[:, :half], field[:, half:]
    lane = lanes(low.shape)
    source = (2 * lane) % half
    return tuple(
        jnp.where(lane < half // 2, take(low, source + odd), take(high, source + odd))
        for odd in (0, 1)
    )


def joined(even, odd):
    half = even.shape[1]
    lane = lanes(even.shape)
    parts = []
    for first in (0, half // 2):
        source = lane // 2 + first
        part = take(even, source)
        if odd is not even:
            part = jnp.where(lane % 2 == 0, part, take(odd, source))
        parts.append(part)
    return jnp.concatenate(parts, axis=1)


def each(function, *fields):
    return tuple(map(function, *fields))


def shift(array, by, axis):
    return pltpu.roll(array, (-by) % array.shape[axis], axis)


def following(field):
    return (*field[1:], shift(field[0], 1, 1))


def preceding(field):
    return (shift(field[-1], -1, 1), *field[:-1])


def laplace(field, by):
    return each(
        lambda c, n, p: (shift(c, by, 0) + shift(c, -by, 0)) + (n + p) - 4.0 * c,
        field,
        following(field),
        preceding(field),
    )


def advance(prey, predator, prey_mob, pred_mob, inv_capacity, scales):
    step_dt, inv_h2 = scales
    by = 3 - len(prey)
    spread_prey = laplace(each(jnp.multiply, prey_mob, prey), by)
    spread_pred = laplace(each(jnp.multiply, pred_mob, predator), by)

    def flux(prey_here, pred_here, prey_next, pred_next):
        return (pred_here + pred_next) * (prey_next - prey_here)

    rows_on = [each(lambda c: shift(c, by, 0), field) for field in (prey, predator)]
    row_flux = each(flux, prey, predator, *rows_on)
    col_flux = each(flux, prey, predator, following(prey), following(predator))
    taxis_div = each(
        lambda r, c, p: (r - shift(r, -by, 0)) + (c - p), row_flux, col_flux, preceding(col_flux)
    )
    response = each(lambda u, v: u * v / (1.0 + HANDLING * jnp.abs(u)), prey, predator)
    new_prey = each(
        lambda u, s, k, r: (
            u + s + (step_dt * GROWTH) * (u * (1.0 - u * k)) - (step_dt * ATTACK) * r
        ),
        prey,
        spread_prey,
        inv_capacity,
        response,
    )
    new_pred = each(
        lambda v, s, d, r: (
            (1.0 - step_dt * MORTALITY) * v
            + s
            - (0.5 * TAXIS * step_dt * inv_h2) * d
            + (step_dt * CONVERSION * ATTACK) * r
        ),
        predator,
        spread_pred,
        taxis_div,
        response,
    )
    return new_prey, new_pred


def restrict(field):
    even, odd = field
    total = even + odd
    row = lax.broadcasted_iota(jnp.int32, total.shape, 0)
    partner = jnp.where(row % 2 == 0, shift(total, 1, 0), shift(total, -1, 0))
    return ((total + partner) * 0.25,)


def edge_tile(strip):
    head = lax.broadcasted_iota(jnp.int32, (TILE, strip.shape[1]), 0) < EDGE
    return jnp.where(head, strip[:TILE], strip[strip.shape[0] - TILE :])


def halo(after, before, swapped):
    head = lax.broadcasted_iota(jnp.int32, after.shape, 0) < EDGE
    if swapped:
        head = head == (lax.axis_index("space") % 2 == 0)
    return jnp.where(head, after, before)


def halves(array):
    half = array.shape[-1] // 2
    return array[:, :half], array[:, half:]


def load_kernel(starts_hbm, habitat_hbm, edges_ref, strip_ref, starts_ref, habitat_ref, sem):
    copies = [
        pltpu.make_async_copy(starts_hbm, starts_ref, sem.at[0]),
        pltpu.make_async_copy(habitat_hbm, habitat_ref, sem.at[1]),
    ]
    for copy in copies:
        copy.start()
    for copy in copies:
        copy.wait()
    fields = [starts_ref[0, 0], starts_ref[0, 1], habitat_ref[...].astype(jnp.float32)]
    for k, field in enumerate(fields):
        edges_ref[k] = jnp.concatenate(split(edge_tile(field)), axis=1)
        strip_ref[k] = field


def lookups(tables, habitat):
    index = habitat.astype(jnp.int32)
    return [take(jnp.broadcast_to(table[:1], index.shape), index) for table in tables]


def prepare_kernel(strip_ref, prey_ref, pred_ref, cap_ref, fields_ref, coefs_ref, tables_ref):
    lane = lanes(tables_ref.shape[1:])
    tables = []
    for ref in (prey_ref, pred_ref, cap_ref):
        table = jnp.full(lane.shape, ref[0], jnp.float32)
        for klass in range(1, ref.shape[0]):
            table = jnp.where(lane == klass, ref[klass], table)
        tables.append(table)
    tables.append(1.0 / tables[2])
    for k, table in enumerate(tables):
        tables_ref[k] = table
    half = fields_ref.shape[2] // 2
    for k in range(2):
        fields_ref[k] = jnp.concatenate(split(strip_ref[k]), axis=1)
    for part, habitat in enumerate(split(strip_ref[2])):
        for k, coef in enumerate(lookups(tables, habitat)):
            coefs_ref[k, :, part * half : (part + 1) * half] = coef


def propagate_kernel(
    fields_ref,
    coefs_ref,
    tables_ref,
    after_ref,
    before_ref,
    coarse_end_ref,
    coarse_coefs_ref,
    coarse_correction_ref,
    correction_ref,
    end_ref,
    *,
    swapped,
):
    def wide(strip, edge):
        return each(lambda *parts: jnp.concatenate(parts, axis=0), halves(strip), halves(edge))

    edges = [halo(after_ref[k], before_ref[k], swapped) for k in range(3)]
    prey, predator = (wide(fields_ref[k], edges[k]) for k in range(2))
    tables = [tables_ref[k] for k in range(4)]
    edge_coefs = zip(*(lookups(tables, part) for part in halves(edges[2])))
    coefs = [
        wide(coefs_ref[k], jnp.concatenate(edge, axis=1)) for k, edge in enumerate(edge_coefs)
    ]
    prey_mob, pred_mob, capacity, inv_capacity = coefs
    scale = COARSE[0] * COARSE[1]
    coarse_coefs = (
        each(lambda c: scale * c, restrict(prey_mob)),
        each(lambda c: scale * c, restrict(pred_mob)),
        each(lambda c: 1.0 / c, restrict(capacity)),
    )
    coarse = advance(restrict(prey), restrict(predator), *coarse_coefs, COARSE)
    fine = prey, predator
    for _ in range(2):
        fine = advance(*fine, prey_mob, pred_mob, inv_capacity, FINE)
    rows = fields_ref.shape[1]
    for k in range(2):
        correction = each(lambda f: f - coarse[k][0], fine[k])
        end = each(lambda c: coarse[k][0] + c, correction)
        coarse_end_ref[k] = restrict(end)[0]
        coarse_correction_ref[k] = restrict(correction)[0][:rows]
        correction_ref[k] = jnp.concatenate(correction, axis=1)[:rows]
        end_ref[k] = jnp.concatenate(end, axis=1)[:rows]
    for k in range(3):
        coarse_coefs_ref[k] = coarse_coefs[k][0]


def natural_kernel(correction_ref, end_ref, correction_out_ref, end_out_ref):
    for source, target in ((correction_ref, correction_out_ref), (end_ref, end_out_ref)):
        for k in range(2):
            target[0, k] = joined(*halves(source[k]))


def hand_kernel(
    arrived_ref,
    coarse_coefs_ref,
    coarse_correction_ref,
    correction_ref,
    end_ref,
    out_ref,
    *coarse_out_ref,
    taker,
):
    rows = correction_ref.shape[2]
    coarse = advance(
        *((arrived_ref[k],) for k in range(2)), *((coarse_coefs_ref[k],) for k in range(3)), COARSE
    )
    takes = lax.axis_index("tm") == taker
    for k in range(2):
        handed = coarse[k][0][:rows]
        out_ref[0, k] = jnp.where(
            takes, joined(handed, handed) + correction_ref[0, k], end_ref[0, k]
        )
        for ref in coarse_out_ref:
            ref[k] = handed + coarse_correction_ref[k]


def edges_kernel(strip_ref, out_ref):
    for k in range(strip_ref.shape[0]):
        out_ref[k] = edge_tile(strip_ref[k])


def widen_kernel(strip_ref, after_ref, before_ref, out_ref, *, swapped):
    for k in range(strip_ref.shape[0]):
        edge = halo(after_ref[k], before_ref[k], swapped)
        out_ref[k] = jnp.concatenate([strip_ref[k], edge], axis=0)


def local_call(kernel, outs, arrays, tables=(), space=pltpu.VMEM, scratch=()):
    vmem, smem = pl.BlockSpec(memory_space=pltpu.VMEM), pl.BlockSpec(memory_space=pltpu.SMEM)
    return pl.pallas_call(
        kernel,
        out_shape=[jax.ShapeDtypeStruct(shape, jnp.float32) for shape in outs],
        in_specs=[pl.BlockSpec(memory_space=space)] * len(arrays) + [smem] * len(tables),
        out_specs=[vmem] * len(outs),
        scratch_shapes=scratch,
        compiler_params=pltpu.CompilerParams(vmem_limit_bytes=4 * 2**20),
    )(*arrays, *tables)


def both_neighbours(tile):
    count = lax.axis_size("space")
    ring = [(i, (i + 1) % count) for i in range(count)]
    if count % 2:
        return (
            lax.ppermute(tile, "space", [(j, i) for i, j in ring]),
            lax.ppermute(tile, "space", ring),
            False,
        )
    swaps = [[pair for i, j in ring[start::2] for pair in ((i, j), (j, i))] for start in (0, 1)]
    outer = lax.ppermute(tile, "space", swaps[1])
    inner = lax.ppermute(tile, "space", swaps[0])
    return inner, outer, True


def from_behind(array):
    count = lax.axis_size("tm")
    return lax.ppermute(array, "tm", [(i, (i + 1) % count) for i in range(count)])


def on_device(slice_starts, habitat, capacity_table, prey_motility, predator_motility):
    _, fields, rows, columns = slice_starts.shape
    wide, half = rows + TILE, columns // 2
    slices = lax.axis_size("tm")
    edges, strip = local_call(
        load_kernel,
        [(3, TILE, columns), (3, rows, columns)],
        [pltpu.with_memory_space_constraint(a, pltpu.HBM) for a in (slice_starts, habitat)],
        space=pltpu.HBM,
        scratch=[
            pltpu.VMEM(slice_starts.shape, slice_starts.dtype),
            pltpu.VMEM(habitat.shape, habitat.dtype),
            pltpu.SemaphoreType.DMA((2,)),
        ],
    )
    after, before, swapped = both_neighbours(edges)
    prepared = local_call(
        prepare_kernel,
        [(fields, rows, columns), (4, rows, columns), (4, TILE, half)],
        [strip],
        [prey_motility, predator_motility, capacity_table],
    )
    coarse_end, coarse_coefs, coarse_correction, correction, end = local_call(
        functools.partial(propagate_kernel, swapped=swapped),
        [
            (fields, wide, half),
            (3, wide, half),
            (fields, rows, half),
            (fields, rows, columns),
            (fields, rows, columns),
        ],
        [*prepared, after, before],
    )
    correction, end = local_call(
        natural_kernel, [slice_starts.shape, slice_starts.shape], [correction, end]
    )
    for taker in range(1, slices):
        arrived = from_behind(coarse_end)
        if taker > 1:
            (edges,) = local_call(edges_kernel, [(fields, TILE, half)], [arrived])
            after, before, swapped = both_neighbours(edges)
            (arrived,) = local_call(
                functools.partial(widen_kernel, swapped=swapped),
                [(fields, wide, half)],
                [arrived, after, before],
            )
        last = taker + 1 == slices
        end, *passed = local_call(
            functools.partial(hand_kernel, taker=taker),
            [slice_starts.shape] + [(fields, rows, half)] * (not last),
            [arrived, coarse_coefs, coarse_correction, correction, end],
        )
        coarse_end = None if last else passed[0]
    return end


def solution(mesh):
    placed = (P("tm", None, "space", None), P("space", None), P(), P(), P())
    return jax.shard_map(
        on_device,
        mesh=mesh,
        in_specs=placed,
        out_specs=P("tm", None, "space", None),
        check_vma=False,
    )
```
